32 devices in a mesh: row: 4 (over y, x), col: 8 (over z, core).
Axes of the slice: x: 2, y: 2, z: 4, core: 2. Of those that a mesh axis runs over, the one named last changes fastest.
Arguments:
- chol_factor: bfloat16 [32768, 32768], P('row', 'col')
- normals: bfloat16 [512, 32768], P('row', 'col'), may hold values from -6 to 6
- site_median: float32 [32768], P(('row', 'col')), may hold values from -3 to 3
- site_region: int32 [32768, 1], replicated, may hold values from 0 to 31; in each aligned block of 1024 rows (0 to 1023, 1024 to 2047, ...) at most 64 rows name the same one
- asset_pick: int32 [131072], P(('row', 'col')), may hold values from 0 to 65535
- asset_zone: int32 [131072], P(('row', 'col')), may hold values from 0 to 4095, as said below
- asset_capacity: float32 [131072], P(('row', 'col')), may hold values from -1.5 to 1.5
- asset_beta: float32 [131072], P(('row', 'col')), may hold values from 0.3 to 0.8
- asset_value: float32 [131072], P(('row', 'col')), may hold values from 0.005 to 0.05
Outputs:
- zone_loss: float32 [4096, 512], P(('row', 'col'))
The draws below stay inside these ranges and needn't reach their ends.
Inputs may be any that keep to these rules, and one draw needn't show every extreme that they name: `site_region`: every region has at least one site; within each aligned block of 1024 sites no region has more than 64 sites, and some region has exactly 64. `asset_zone`: within each aligned block of 4096 assets, exactly 128 assets fall in each aligned run of 128 zones.
All inputs are finite; a program needn't handle non-finite values.
Results may differ from the reference program's by a relative error of at most 0.0012.
Values may be sent and summed in bfloat16 or wider, within the bound.
A program may use at most 128 MiB of HBM per device.

```python
import math
import jax
import jax.numpy as jnp
import numpy as np
from jax import lax

NS = 32768
EVENTS = 512
ASSET_DEV = 4096
ZONES = 4096
SITE_DEV = 1024
CAP = 64
ASSETS = 131072
N_ROW = 4
DEVICES = 32


def draw_chol_factor(key, part):
    rows_idx = jnp.arange(NS, dtype=jnp.int32)[:, None]
    cols_idx = jnp.arange(NS, dtype=jnp.int32)[None, :]
    offdiag = jax.random.normal(jax.random.fold_in(key, 3), (NS, NS), jnp.float32)
    offdiag = offdiag * jax.lax.rsqrt(rows_idx.astype(jnp.float32) + 1.0)
    diagonal = jax.random.uniform(jax.random.fold_in(key, 5), (NS, NS), jnp.float32, 0.5, 1.0)
    factor = jnp.where(cols_idx < rows_idx, offdiag, jnp.where(cols_idx == rows_idx, diagonal, 0.0))
    return factor.astype(jnp.bfloat16)


def draw_asset_zone(key, part):
    keys = jax.random.split(jax.random.fold_in(key, 11), DEVICES)
    orders = jax.vmap(lambda subkey: jax.random.permutation(subkey, ASSET_DEV))(keys)
    owners = orders // (ASSET_DEV // DEVICES)
    inner = jax.random.randint(jax.random.fold_in(key, 12), (DEVICES, ASSET_DEV), 0, ZONES // DEVICES)
    return (owners * (ZONES // DEVICES) + inner).reshape(-1).astype(jnp.int32)


def place_ends(result, rng, smallest, top_value):
    dims = result.shape
    spot = [jax.random.randint(jax.random.fold_in(rng, axis), (), 0, dims[axis]) for axis in range(len(dims))]
    result = result.at[tuple(spot)].set(smallest)
    longest = dims.index(max(dims))
    spot[longest] = (spot[longest] + 1) % dims[longest]
    return result.at[tuple(spot)].set(top_value)


def shard_levels(key, shape, shards, least, top_value):
    def one(dim, parts):
        steps = jax.random.uniform(jax.random.fold_in(jax.random.fold_in(key, 6), dim), (parts,), jnp.float32, least / len(shards), top_value / len(shards))
        return jnp.repeat(jnp.exp(steps), shape[dim] // parts).reshape((-1,) + (1,) * (len(shape) - dim - 1))

    factor_of = one(*shards[0])
    for cut in shards[1:]:
        factor_of = factor_of * one(*cut)
    return factor_of


def shared_out(rng, own, number, rows, count, top, most, slope):
    sequence = jax.random.permutation(rng, count)
    heavy_load, usual = load_shares(count, rows * top, most, slope, True), load_shares(count, rows * top, most, slope, False)
    places = jnp.arange(count)

    def named(lengths, rotation):
        used = int((lengths > 0).sum())
        fixed = max(1, used // 4)
        moved = fixed + (places - fixed + rotation * (used - fixed)) % max(1, count - fixed)
        return jnp.zeros((count,), jnp.int32).at[sequence[jnp.where(places < fixed, places, moved)]].set(jnp.asarray(lengths, jnp.int32))

    lengths = jnp.where(number % 4 == 0, named(heavy_load, number // 4), named(usual, number - number // 4 - 1))
    mixed = jax.random.permutation(jax.random.fold_in(own, 3), count)
    donor, taker = mixed[0:count // 2 * 2:2], mixed[1:count // 2 * 2:2]
    room = jnp.minimum(lengths[donor] - 1, most - lengths[taker]) // 2
    room = jnp.where((donor == sequence[0]) | (taker == sequence[0]) | (lengths[taker] == 0), 0, jnp.maximum(room, 0))
    moved = jax.random.randint(jax.random.fold_in(own, 4), (count // 2,), 0, 1 << 20) % (room + 1)
    lengths = lengths.at[donor].add(-moved).at[taker].add(moved)
    labels = jnp.searchsorted(jnp.cumsum(lengths), jnp.arange(rows * top), side="right").astype(jnp.int32)
    table = labels.reshape(top, rows).T
    table = table[jax.random.permutation(jax.random.fold_in(own, 1), rows)]
    rotation = jax.random.randint(jax.random.fold_in(own, 2), (rows, 1), 0, top)
    return jnp.take_along_axis(table, (jnp.arange(top)[None, :] + rotation) % top, axis=1)


def load_shares(amount, total, reach, slope, full):
    portions = [(1 << 20) // math.isqrt(standing ** slope) + 1 for standing in range(1, amount + 1)]
    largest = reach if full else min(reach, max(-(-total // amount), total * portions[0] // sum(portions)))
    least = 1 if total - largest >= amount - 1 else 0
    counts, rest = [largest] + [least] * (amount - 1), total - largest - least * (amount - 1)
    while rest > 0:
        free = [i for i in range(1, amount) if counts[i] < largest] or [i for i in range(1, amount) if counts[i] < reach]
        pool, remaining = sum([portions[i] for i in free]), rest
        for i in free:
            extra = min(reach - counts[i], max(1, remaining * portions[i] // pool), rest)
            counts[i] = counts[i] + extra
            rest = rest - extra
    return np.array(counts)


def noise(key, shape, deviation, reach, cuts=(), held_as=jnp.bfloat16):
    array = jax.random.normal(key, shape, jnp.float32) * deviation
    if len(cuts) > 0:
        array = shard_levels(key, shape, cuts, -0.22, 0.18) * array
    return jnp.clip(array, min=-reach, max=reach).astype(held_as)


def setup_inputs(seed: int = 0) -> dict:
    key_of = jax.random.split(jax.random.key(seed), 10)
    chol_factor = draw_chol_factor(jax.random.fold_in(key_of[9], 71), 0)
    normals = noise(key_of[1], (EVENTS, NS), 1.0, 6.0, ((0, 4), (1, 8)))
    site_median = noise(key_of[2], (NS,), 0.5, 3.0, ((0, 32),), jnp.float32)
    site_region_keys = jax.random.split(jax.random.fold_in(key_of[3], 1), NS // SITE_DEV)
    site_region_turns = jax.random.permutation(jax.random.fold_in(key_of[3], 3), NS // SITE_DEV)
    site_region = jax.vmap(lambda own, number: shared_out(jax.random.fold_in(key_of[3], 2), own, number, SITE_DEV, DEVICES, 1, CAP, 2))(site_region_keys, site_region_turns).reshape((NS, 1))
    asset_pick = place_ends(jax.random.randint(key_of[4], (ASSETS,), 0, 65536), jax.random.fold_in(key_of[4], 1), 0, 65535).astype(jnp.int32)
    asset_zone = draw_asset_zone(jax.random.fold_in(key_of[9], 71), 0)
    asset_capacity = jnp.clip(jax.random.uniform(key_of[6], (ASSETS,), jnp.float32, -1.5, 1.5) * shard_levels(key_of[6], (ASSETS,), ((0, 32),), -0.4, 0.0), -1.5, 1.5)
    asset_beta = jnp.clip(0.3 + 0.5 * jax.random.uniform(key_of[7], (ASSETS,), jnp.float32) ** shard_levels(key_of[7], (ASSETS,), ((0, 32),), -0.2, 0.2), 0.3, 0.8)
    asset_value = jnp.clip(jnp.exp(math.log(0.05) - 2.3025851 * jax.random.uniform(key_of[8], (ASSETS,), jnp.float32) ** shard_levels(key_of[8], (ASSETS,), ((0, 32),), -0.2, 0.2)), 0.005, 0.05)
    return dict(chol_factor=chol_factor, normals=normals, site_median=site_median, site_region=site_region, asset_pick=asset_pick, asset_zone=asset_zone, asset_capacity=asset_capacity, asset_beta=asset_beta, asset_value=asset_value)


def normal_cdf(argument):
    return 0.5 * (1.0 + jax.scipy.special.erf(argument * 0.7071067811865476))


def reference(chol_factor, normals, site_median, site_region, asset_pick, asset_zone, asset_capacity, asset_beta, asset_value):
    blocks = chol_factor.reshape(N_ROW, NS // N_ROW, NS)

    def block_field(row_block):
        return lax.dot_general(row_block, normals, (((1,), (1,)), ((), ())), preferred_element_type=jnp.float32)

    field_sum = lax.map(block_field, blocks).reshape(NS, EVENTS)
    log_motion = (site_median[:, None] + field_sum).astype(jnp.bfloat16)
    regions = site_region[:, 0]
    pick_rows = asset_pick.reshape(DEVICES, ASSET_DEV)

    def region_sites(inputs_pair):
        region_id, picked = inputs_pair
        running = jnp.cumsum((regions == region_id).astype(jnp.int32)).astype(jnp.int32)
        chosen = picked % running[-1]
        return jnp.searchsorted(running, chosen + 1, side="left").astype(jnp.int32)

    site_index = lax.map(region_sites, (jnp.arange(DEVICES, dtype=jnp.int32), pick_rows)).reshape(-1)
    motion = log_motion[site_index].astype(jnp.float32)
    damage = (asset_value[:, None] * normal_cdf((motion - asset_capacity[:, None]) / asset_beta[:, None])).astype(jnp.bfloat16)
    return jax.ops.segment_sum(damage.astype(jnp.float32), asset_zone, num_segments=ZONES)
```

```python
import jax
import jax.numpy as jnp
from jax import lax
from jax.experimental import pallas as pl
from jax.experimental.pallas import tpu as pltpu
from jax.sharding import PartitionSpec as P

ZONES = 4096
CHUNKS = 2


def normal_cdf(argument):
    return 0.5 * (1.0 + jax.scipy.special.erf(argument * 0.7071067811865476))


def swap(value, axis, bit):
    size = lax.axis_size(axis)
    return lax.ppermute(value, axis, [(i, i ^ bit) for i in range(size)])


def bits_of(size):
    return [1 << k for k in range(size.bit_length() - 1)]


def gather_rows(block, order):
    me = lax.axis_index("row")
    held = block
    axes = []
    for bit in order:
        other = swap(held, "row", bit)
        low = (me // bit) % 2 == 0
        held = jnp.stack([jnp.where(low, held, other), jnp.where(low, other, held)], axis=0)
        axes.insert(0, bit)
    rank = [axes.index(bit) for bit in sorted(axes, reverse=True)]
    held = held.transpose(tuple(rank) + (len(axes), len(axes) + 1))
    return held.reshape(-1, block.shape[1])


def panel_kernel(side_ref, factor_ref, *refs):
    count = len(refs) // 2
    for panel_ref, out_ref in zip(refs[:count], refs[count:]):
        out_ref[...] = lax.dot_general(
            factor_ref[...],
            panel_ref[...],
            (((1,), (1,)), ((), ())),
            preferred_element_type=jnp.float32,
        ).astype(out_ref.dtype)


def half_field(chol_factor, panels, side, line, block, dtype):
    depth = chol_factor.shape[1]
    tile = min(512, block)
    per_block = block // tile
    panel_specs = [pl.BlockSpec(p.shape, lambda i, j, side: (0, 0)) for p in panels]
    out_specs = [
        pl.BlockSpec((tile, p.shape[0]), lambda i, j, side: (i * per_block + j, 0))
        for p in panels
    ]
    rows = line * block
    events = sum(p.shape[0] for p in panels)
    return pl.pallas_call(
        panel_kernel,
        grid_spec=pltpu.PrefetchScalarGridSpec(
            num_scalar_prefetch=1,
            grid=(line, per_block),
            in_specs=[
                pl.BlockSpec(
                    (tile, depth),
                    lambda i, j, side: ((2 * i + side[0]) * per_block + j, 0),
                )
            ]
            + panel_specs,
            out_specs=out_specs,
        ),
        out_shape=[jax.ShapeDtypeStruct((rows, p.shape[0]), dtype) for p in panels],
        compiler_params=pltpu.CompilerParams(vmem_limit_bytes=48 * 1024 * 1024),
        cost_estimate=pl.CostEstimate(
            flops=2 * rows * depth * events,
            bytes_accessed=2 * rows * depth + 4 * rows * events,
            transcendentals=0,
        ),
    )(side.reshape(1).astype(jnp.int32), chol_factor, *panels)


def field_scatter(mine, theirs):
    me = lax.axis_index("col")
    line = mine.shape[0]
    place = me // 2
    summed = mine + swap(theirs, "col", 1).astype(jnp.float32)
    up = down = None
    for step in range(1, line):
        index_up = jnp.clip(place + line - step, 0, line - 1)
        index_down = jnp.clip(place - line + step, 0, line - 1)
        send_up = lax.dynamic_index_in_dim(summed, index_up, 0, keepdims=False)
        send_down = lax.dynamic_index_in_dim(summed, index_down, 0, keepdims=False)
        if up is not None:
            send_up = send_up + up.astype(jnp.float32)
            send_down = send_down + down.astype(jnp.float32)
        pairs_up, pairs_down = [], []
        for p in range(line):
            for c in range(2):
                if p < step and p + 1 < line:
                    pairs_up.append((2 * p + c, 2 * p + 2 + c))
                if p >= line - step and p > 0:
                    pairs_down.append((2 * p + c, 2 * p - 2 + c))
        up = lax.ppermute(send_up.astype(jnp.bfloat16), "col", pairs_up)
        down = lax.ppermute(send_down.astype(jnp.bfloat16), "col", pairs_down)
    own = lax.dynamic_index_in_dim(summed, place, 0, keepdims=False)
    if up is not None:
        own = own + up.astype(jnp.float32) + down.astype(jnp.float32)
    return own


def zone_scatter(table, order):
    rows, cols = lax.axis_size("row"), lax.axis_size("col")
    dims = [2] * (len(bits_of(rows)) + len(bits_of(cols)))
    row_bits, col_bits = bits_of(rows), bits_of(cols)
    tail = table.shape[1:]
    steps = [("col", 1)] + [("row", b) for b in order] + [("col", b) for b in col_bits[:0:-1]]
    names = [("row", b) for b in row_bits[::-1]] + [("col", b) for b in col_bits[::-1]]
    held = table.reshape(tuple(dims) + tail)
    for number, (axis, bit) in enumerate(steps):
        where = names.index((axis, bit))
        names.pop(where)
        side = (lax.axis_index(axis) // bit) % 2
        give = lax.dynamic_index_in_dim(held, 1 - side, where, keepdims=False)
        keep = lax.dynamic_index_in_dim(held, side, where, keepdims=False)
        if number < len(steps) - 1:
            give = give.astype(jnp.bfloat16)
        held = keep + swap(give, axis, bit).astype(jnp.float32)
    return held


def split3(value):
    high = lax.reduce_precision(value, 8, 7)
    rest = value - high
    middle = lax.reduce_precision(rest, 8, 7)
    return [high, middle, rest - middle]


def per_device(
    chol_factor,
    normals,
    site_median,
    site_region,
    asset_pick,
    asset_zone,
    asset_capacity,
    asset_beta,
    asset_value,
):
    rows, cols = lax.axis_size("row"), lax.axis_size("col")
    device_count = rows * cols
    own_index = lax.axis_index(("row", "col"))
    local_events = normals.shape[0]
    part = local_events // CHUNKS
    row_bits = bits_of(rows)

    gathered = []
    for chunk in range(CHUNKS):
        order = row_bits if chunk % 2 == 0 else row_bits[::-1]
        gathered.append(gather_rows(normals[chunk * part : (chunk + 1) * part], order))

    site_count = site_median.shape[0]
    slot_cap = max(2, 2 * site_count // device_count)
    slots = device_count * slot_cap
    all_regions = site_region[:, 0].reshape(device_count, site_count)
    block_regions = lax.dynamic_index_in_dim(all_regions, own_index, 0, keepdims=False)
    devices = jnp.arange(device_count, dtype=jnp.int32)

    def rank_of(labels):
        count = labels.shape[0]
        steps = jnp.arange(count, dtype=jnp.int32)
        onehot = (labels[:, None] == devices[None, :]).astype(jnp.bfloat16)
        before = (steps[:, None] > steps[None, :]).astype(jnp.bfloat16)
        running = jnp.dot(before, onehot, preferred_element_type=jnp.float32)
        return jnp.sum(running * onehot.astype(jnp.float32), axis=1).astype(jnp.int32)

    position = block_regions * slot_cap + rank_of(block_regions)
    selector = (position[None, :] == jnp.arange(slots, dtype=jnp.int32)[:, None]).astype(
        jnp.bfloat16
    )
    counts = jnp.sum((all_regions == own_index).astype(jnp.int32), axis=1)
    first = jnp.sum(jnp.where(devices[None, :] < devices[:, None], counts[None, :], 0), axis=1)
    slot_steps = jnp.arange(slot_cap, dtype=jnp.int32)[None, :]
    slot_rank = jnp.where(
        slot_steps < counts[:, None], first[:, None] + slot_steps, -1
    ).reshape(-1)
    total = jnp.sum(counts)

    assets = asset_pick.shape[0]
    zone_share = ZONES // device_count
    per_owner = assets // device_count
    zone_owner = asset_zone // zone_share
    placing = zone_owner * per_owner + rank_of(zone_owner)
    chosen = asset_pick % total
    table = jnp.stack(
        split3(asset_capacity)
        + split3(asset_beta)
        + split3(asset_value)
        + [
            (chosen // 256).astype(jnp.float32),
            (chosen % 256).astype(jnp.float32),
            (asset_zone % zone_share).astype(jnp.float32),
        ],
        axis=1,
    ).astype(jnp.bfloat16)
    order_of = (placing[None, :] == jnp.arange(assets, dtype=jnp.int32)[:, None]).astype(
        jnp.bfloat16
    )
    placed = jnp.dot(order_of, table, preferred_element_type=jnp.float32)
    capacity = placed[:, 0] + placed[:, 1] + placed[:, 2]
    beta = placed[:, 3] + placed[:, 4] + placed[:, 5]
    value = placed[:, 6] + placed[:, 7] + placed[:, 8]
    pick = (placed[:, 9] * 256.0 + placed[:, 10]).astype(jnp.int32)
    inner_zone = placed[:, 11].astype(jnp.int32).reshape(device_count, per_owner)
    member = (
        inner_zone[:, None, :] == jnp.arange(zone_share, dtype=jnp.int32)[None, :, None]
    ).astype(jnp.bfloat16)
    chooser = (pick[:, None] == slot_rank[None, :]).astype(jnp.bfloat16)

    line, core = cols // 2, lax.axis_index("col") % 2
    theirs = half_field(chol_factor, gathered, 1 - core, line, site_count, jnp.bfloat16)
    mine = half_field(chol_factor, gathered, core, line, site_count, jnp.float32)

    results = []
    for chunk in range(CHUNKS):
        shape = (line, site_count, rows * part)
        field = field_scatter(mine[chunk].reshape(shape), theirs[chunk].reshape(shape))
        log_motion = (site_median[:, None] + field).astype(jnp.bfloat16)
        events = log_motion.shape[1]
        outgoing = jnp.dot(selector, log_motion, preferred_element_type=jnp.float32).astype(
            jnp.bfloat16
        )
        incoming = lax.all_to_all(
            outgoing.reshape(device_count, slot_cap, events),
            ("row", "col"),
            split_axis=0,
            concat_axis=0,
            tiled=True,
        ).reshape(slots, events)
        motion = jnp.dot(chooser, incoming, preferred_element_type=jnp.float32)
        damage = (
            value[:, None] * normal_cdf((motion - capacity[:, None]) / beta[:, None])
        ).astype(jnp.bfloat16)
        zone_table = jnp.einsum(
            "dzp,dpe->dze",
            member,
            damage.reshape(device_count, per_owner, events),
            preferred_element_type=jnp.float32,
        )
        order = row_bits if chunk % 2 == 0 else row_bits[::-1]
        zones = zone_scatter(zone_table, order)
        results.append(zones.reshape(zone_share, rows, part))
    return jnp.stack(results, axis=2).reshape(zone_share, rows * local_events)


def solution(mesh):
    in_specs = (
        P("row", "col"),
        P("row", "col"),
        P(("row", "col")),
        P(),
        P(("row", "col")),
        P(("row", "col")),
        P(("row", "col")),
        P(("row", "col")),
        P(("row", "col")),
    )
    out_specs = P(("row", "col"), None)
    return jax.shard_map(
        per_device, mesh=mesh, in_specs=in_specs, out_specs=out_specs, check_vma=False
    )
```

```python
import jax
import jax.numpy as jnp
from jax import lax
from jax.experimental import pallas as pl
from jax.experimental.pallas import tpu as pltpu
from jax.sharding import PartitionSpec as P

ZONES = 4096
CHUNKS = 2


def normal_cdf(argument):
    return 0.5 * (1.0 + jax.scipy.special.erf(argument * 0.7071067811865476))


def swap(value, axis, bit):
    size = lax.axis_size(axis)
    return lax.ppermute(value, axis, [(i, i ^ bit) for i in range(size)])


def bits_of(size):
    return [1 << k for k in range(size.bit_length() - 1)]


def gather_rows(block, order):
    me = lax.axis_index("row")
    held = block
    axes = []
    for bit in order:
        other = swap(held, "row", bit)
        low = (me // bit) % 2 == 0
        held = jnp.stack([jnp.where(low, held, other), jnp.where(low, other, held)], axis=0)
        axes.insert(0, bit)
        if len(axes) == 1:
            held = yield held
    rank = [axes.index(bit) for bit in sorted(axes, reverse=True)]
    held = held.transpose(tuple(rank) + (len(axes), len(axes) + 1))
    yield held.reshape(-1, block.shape[1])


def panel_kernel(side_ref, factor_ref, *refs):
    count = len(refs) // 2
    for panel_ref, out_ref in zip(refs[:count], refs[count:]):
        out_ref[...] = lax.dot_general(
            factor_ref[...],
            panel_ref[...],
            (((1,), (1,)), ((), ())),
            preferred_element_type=jnp.float32,
        ).astype(out_ref.dtype)


def send_order(line):
    return [sorted(range(line), key=lambda b: (-abs(b - p), -b)) for p in range(line)]


def block_field(chol_factor, panels, blocks, block, dtype):
    depth = chol_factor.shape[1]
    tile = min(512, block)
    per_block = block // tile
    panel_specs = [pl.BlockSpec(p.shape, lambda i, j, which: (0, 0)) for p in panels]
    out_specs = [
        pl.BlockSpec((tile, p.shape[0]), lambda i, j, which: (i * per_block + j, 0))
        for p in panels
    ]
    count = blocks.shape[0]
    rows = count * block
    events = sum(p.shape[0] for p in panels)
    outs = pl.pallas_call(
        panel_kernel,
        grid_spec=pltpu.PrefetchScalarGridSpec(
            num_scalar_prefetch=1,
            grid=(count, per_block),
            in_specs=[
                pl.BlockSpec((tile, depth), lambda i, j, which: (which[i] * per_block + j, 0))
            ]
            + panel_specs,
            out_specs=out_specs,
        ),
        out_shape=[jax.ShapeDtypeStruct((rows, p.shape[0]), dtype) for p in panels],
        compiler_params=pltpu.CompilerParams(vmem_limit_bytes=48 * 1024 * 1024),
        cost_estimate=pl.CostEstimate(
            flops=2 * rows * depth * events,
            bytes_accessed=2 * rows * depth + 4 * rows * events,
            transcendentals=0,
        ),
    )(blocks.astype(jnp.int32), chol_factor, *panels)
    return [o.reshape(count, block, o.shape[1]) for o in outs]


def field_scatter(mine, theirs):
    me = lax.axis_index("col")
    line = sum(m.shape[0] for m in mine)
    first = mine[0].shape[0]
    place = me // 2
    order = send_order(line)
    where = [[order[p].index(b) for b in range(line)] for p in range(line)]
    summed = [m + swap(t, "col", 1).astype(jnp.float32) for m, t in zip(mine, theirs)]

    def take(wanted):
        spots = [where[p][b] if b is not None else 0 for p, b in enumerate(wanted)]
        spot = sum(jnp.where(place == p, k, 0) for p, k in enumerate(spots))
        early = lax.dynamic_index_in_dim(
            summed[0], jnp.minimum(spot, first - 1), 0, keepdims=False
        )
        if max(spots) < first:
            return early
        late = lax.dynamic_index_in_dim(
            summed[1], jnp.maximum(spot - first, 0), 0, keepdims=False
        )
        if min(spots) >= first:
            return late
        return jnp.where(spot < first, early, late)

    up = down = None
    for step in range(1, line):
        reach = line - step
        blocks_up = [p + reach if p + reach < line else None for p in range(line)]
        blocks_down = [p - reach if p - reach >= 0 else None for p in range(line)]
        send_up, send_down = take(blocks_up), take(blocks_down)
        if up is not None:
            send_up = send_up + up.astype(jnp.float32)
            send_down = send_down + down.astype(jnp.float32)
        pairs_up, pairs_down = [], []
        for p in range(line):
            for c in range(2):
                if blocks_up[p] is not None:
                    pairs_up.append((2 * p + c, 2 * p + 2 + c))
                if blocks_down[p] is not None:
                    pairs_down.append((2 * p + c, 2 * p - 2 + c))
        up = lax.ppermute(send_up.astype(jnp.bfloat16), "col", pairs_up)
        down = lax.ppermute(send_down.astype(jnp.bfloat16), "col", pairs_down)
    own = take(list(range(line)))
    if up is not None:
        own = own + up.astype(jnp.float32) + down.astype(jnp.float32)
    return own


def zone_scatter(table, order):
    rows, cols = lax.axis_size("row"), lax.axis_size("col")
    dims = [2] * (len(bits_of(rows)) + len(bits_of(cols)))
    row_bits, col_bits = bits_of(rows), bits_of(cols)
    tail = table.shape[1:]
    steps = [("col", 1)] + [("row", b) for b in order] + [("col", b) for b in col_bits[:0:-1]]
    names = [("row", b) for b in row_bits[::-1]] + [("col", b) for b in col_bits[::-1]]
    held = table.reshape(tuple(dims) + tail)
    for number, (axis, bit) in enumerate(steps):
        where = names.index((axis, bit))
        names.pop(where)
        side = (lax.axis_index(axis) // bit) % 2
        give = lax.dynamic_index_in_dim(held, 1 - side, where, keepdims=False)
        keep = lax.dynamic_index_in_dim(held, side, where, keepdims=False)
        if number < len(steps) - 2:
            give = give.astype(jnp.bfloat16)
        held = keep + swap(give, axis, bit).astype(jnp.float32)
        if number == 1:
            held = yield held
    yield held


def split3(value):
    high = lax.reduce_precision(value, 8, 7)
    rest = value - high
    middle = lax.reduce_precision(rest, 8, 7)
    return [high, middle, rest - middle]


def per_device(
    chol_factor,
    normals,
    site_median,
    site_region,
    asset_pick,
    asset_zone,
    asset_capacity,
    asset_beta,
    asset_value,
):
    rows, cols = lax.axis_size("row"), lax.axis_size("col")
    device_count = rows * cols
    own_index = lax.axis_index(("row", "col"))
    local_events = normals.shape[0]
    part = local_events // CHUNKS
    row_bits = bits_of(rows)

    gathered = []
    for chunk in range(CHUNKS):
        order = row_bits if chunk % 2 == 0 else row_bits[::-1]
        gathered.append(gather_rows(normals[chunk * part : (chunk + 1) * part], order))
    starts, asset_zone, site_region = lax.optimization_barrier(
        ([next(g) for g in gathered], asset_zone, site_region)
    )
    gathered = [g.send(start) for g, start in zip(gathered, starts)]

    site_count = site_median.shape[0]
    slot_cap = max(2, 2 * site_count // device_count)
    slots = device_count * slot_cap
    all_regions = site_region[:, 0].reshape(device_count, site_count)
    block_regions = lax.dynamic_index_in_dim(all_regions, own_index, 0, keepdims=False)
    devices = jnp.arange(device_count, dtype=jnp.int32)

    def rank_of(labels):
        count = labels.shape[0]
        steps = jnp.arange(count, dtype=jnp.int32)
        onehot = (labels[:, None] == devices[None, :]).astype(jnp.bfloat16)
        before = (steps[:, None] > steps[None, :]).astype(jnp.bfloat16)
        running = jnp.dot(before, onehot, preferred_element_type=jnp.float32)
        return jnp.sum(running * onehot.astype(jnp.float32), axis=1).astype(jnp.int32)

    position = block_regions * slot_cap + rank_of(block_regions)
    selector = (position[None, :] == jnp.arange(slots, dtype=jnp.int32)[:, None]).astype(
        jnp.bfloat16
    )
    counts = jnp.sum((all_regions == own_index).astype(jnp.int32), axis=1)
    first = jnp.sum(jnp.where(devices[None, :] < devices[:, None], counts[None, :], 0), axis=1)
    slot_steps = jnp.arange(slot_cap, dtype=jnp.int32)[None, :]
    slot_rank = jnp.where(
        slot_steps < counts[:, None], first[:, None] + slot_steps, -1
    ).reshape(-1)
    total = jnp.sum(counts)

    assets = asset_pick.shape[0]
    zone_share = ZONES // device_count
    per_owner = assets // device_count
    zone_owner = asset_zone // zone_share
    placing = zone_owner * per_owner + rank_of(zone_owner)
    chosen = asset_pick % total
    table = jnp.stack(
        split3(asset_capacity)
        + split3(asset_beta)
        + split3(asset_value)
        + [
            (chosen // 256).astype(jnp.float32),
            (chosen % 256).astype(jnp.float32),
            (asset_zone % zone_share).astype(jnp.float32),
        ],
        axis=1,
    ).astype(jnp.bfloat16)
    order_of = (placing[None, :] == jnp.arange(assets, dtype=jnp.int32)[:, None]).astype(
        jnp.bfloat16
    )
    placed = jnp.dot(order_of, table, preferred_element_type=jnp.float32)
    gathered, slot_rank, placed, selector = lax.optimization_barrier(
        (gathered, slot_rank, placed, selector)
    )
    capacity = placed[:, 0] + placed[:, 1] + placed[:, 2]
    beta = placed[:, 3] + placed[:, 4] + placed[:, 5]
    value = placed[:, 6] + placed[:, 7] + placed[:, 8]
    pick = (placed[:, 9] * 256.0 + placed[:, 10]).astype(jnp.int32)
    inner_zone = placed[:, 11].astype(jnp.int32).reshape(device_count, per_owner)
    member = (
        inner_zone[:, None, :] == jnp.arange(zone_share, dtype=jnp.int32)[None, :, None]
    ).astype(jnp.bfloat16)
    chooser = (pick[:, None] == slot_rank[None, :]).astype(jnp.bfloat16)

    line, me = cols // 2, lax.axis_index("col")
    core = me % 2
    table_of = jnp.asarray(send_order(line), jnp.int32)
    blocks = lax.dynamic_index_in_dim(table_of, me // 2, 0, keepdims=False)
    first = (line + 1) // 2
    theirs, mine = [], []
    for half in (blocks[:first], blocks[first:]):
        if half.shape[0] > 0:
            theirs.append(
                block_field(chol_factor, gathered, 2 * half + 1 - core, site_count, jnp.bfloat16)
            )
            mine.append(
                block_field(chol_factor, gathered, 2 * half + core, site_count, jnp.float32)
            )

    fields = [
        field_scatter([m[chunk] for m in mine], [t[chunk] for t in theirs])
        for chunk in range(CHUNKS)
    ]
    results = []
    for chunk in range(CHUNKS):
        field = fields[chunk]
        log_motion = (site_median[:, None] + field).astype(jnp.bfloat16)
        events = log_motion.shape[1]
        outgoing = jnp.dot(selector, log_motion, preferred_element_type=jnp.float32).astype(
            jnp.bfloat16
        )
        incoming = lax.all_to_all(
            outgoing.reshape(device_count, slot_cap, events),
            ("row", "col"),
            split_axis=0,
            concat_axis=0,
            tiled=True,
        ).reshape(slots, events)
        motion = jnp.dot(chooser, incoming, preferred_element_type=jnp.float32)
        damage = (
            value[:, None] * normal_cdf((motion - capacity[:, None]) / beta[:, None])
        ).astype(jnp.bfloat16)
        zone_table = jnp.einsum(
            "dzp,dpe->dze",
            member,
            damage.reshape(device_count, per_owner, events),
            preferred_element_type=jnp.float32,
        )
        order = row_bits if chunk % 2 == 0 else row_bits[::-1]
        steps = zone_scatter(zone_table, order)
        zones = next(steps)
        if chunk + 1 < CHUNKS:
            zones, fields[chunk + 1] = lax.optimization_barrier((zones, fields[chunk + 1]))
        zones = steps.send(zones)
        results.append(zones.reshape(zone_share, rows, part))
    return jnp.stack(results, axis=2).reshape(zone_share, rows * local_events)


def solution(mesh):
    in_specs = (
        P("row", "col"),
        P("row", "col"),
        P(("row", "col")),
        P(),
        P(("row", "col")),
        P(("row", "col")),
        P(("row", "col")),
        P(("row", "col")),
        P(("row", "col")),
    )
    out_specs = P(("row", "col"), None)
    return jax.shard_map(
        per_device, mesh=mesh, in_specs=in_specs, out_specs=out_specs, check_vma=False
    )
```
